256 devices in a mesh: gx: 16 (over z_lo, x), gy: 16 (over z_hi, y, core).
Axes of the slice: x: 4, y: 4, z: 8 (z_hi: 2, z_lo: 4; z = z_hi * 4 + z_lo), core: 2. Of those that a mesh axis runs over, the one named last changes fastest.
Arguments:
- maps: bfloat16 [16, 16, 2048, 2048], P('gx', 'gy'), may hold values from -0.125 to 0.125
- sources: float32 [16, 16, 256, 2048], P('gx', 'gy'), may hold values from -6 to 6
- traces: bfloat16 [16, 16, 256, 2048], P('gx', 'gy'), may hold values from -6 to 6
Outputs:
- outgoing: bfloat16 [16, 16, 256, 2048], P('gx', 'gy')
The draws below stay inside these ranges and needn't reach their ends.
All inputs are finite; a program needn't handle non-finite values.
Results may differ from the reference program's by a relative error of at most 0.0085.
Values may be sent and summed in bfloat16 or wider, within the bound.
No kernel may reach another device: no remote copies, remote signals or barrier semaphores. Data moves between devices by JAX's collectives and lax.ppermute only.
A program may use at most 64 MiB of HBM per device.

```python
import jax
import jax.numpy as jnp
from jax import lax

FACE = 512
MAPN = 2048
RHS = 256
TICKS = 8
PX = 16
PY = 16


def steps_of(stream_key, shape, cuts, least, top_value):
    gain = 1.0
    for dim, parts in cuts:
        draws = jax.random.uniform(jax.random.fold_in(jax.random.fold_in(stream_key, 6), dim), (parts,), jnp.float32, least / len(cuts), top_value / len(cuts))
        gain = gain * jnp.repeat(jnp.exp(draws), shape[dim] // parts).reshape((-1,) + (1,) * (len(shape) - 1 - dim))
    return gain


def scatter_about(own_key, shape, spread, bound, split=(), held_as=jnp.bfloat16):
    values = jax.random.normal(own_key, shape, jnp.float32) * spread
    if len(split) > 0:
        values = steps_of(own_key, shape, split, -0.22, 0.18) * values
    return jnp.clip(values, min=-bound, max=bound).astype(held_as)


def setup_inputs(seed: int = 0) -> dict:
    splits = jax.random.split(jax.random.key(seed), 4)
    return {
        "maps": scatter_about(splits[0], (PX, PY, MAPN, MAPN), MAPN ** -0.5, 0.125, ((0, 16), (1, 16))),
        "sources": scatter_about(splits[1], (PX, PY, RHS, MAPN), 1.0, 6.0, ((0, 16), (1, 16)), jnp.float32),
        "traces": scatter_about(splits[2], (PX, PY, RHS, MAPN), 1.0, 6.0, ((0, 16), (1, 16))),
    }


def products(state, maps, sources, low, width):
    def one(items):
        block, matrix, source = items
        value = jnp.dot(block, matrix[:, low:low + width], preferred_element_type=jnp.float32)
        return (value + source[:, low:low + width]).astype(jnp.bfloat16)

    def flat(array):
        return array.reshape((PX * PY,) + array.shape[2:])

    result = lax.map(one, (flat(state), flat(maps), flat(sources)))
    return result.reshape((PX, PY) + result.shape[1:])


def reference(maps, sources, traces):
    face = FACE
    state = traces
    for tick in range(TICKS):
        if tick == TICKS - 1:
            return products(state, maps, sources, 0, 4 * face)
        if tick < TICKS // 2:
            faces = products(state, maps, sources, 2 * face, 2 * face)
            east = faces[..., :face]
            north = faces[..., face:]
            west_new = jnp.concatenate([jnp.zeros_like(east[:1]), east[:-1]], axis=0)
            south_new = jnp.concatenate([jnp.zeros_like(north[:, :1]), north[:, :-1]], axis=1)
            state = jnp.concatenate([west_new, south_new, state[..., 2 * face:]], axis=-1)
        else:
            faces = products(state, maps, sources, 0, 2 * face)
            west = faces[..., :face]
            south = faces[..., face:]
            east_new = jnp.concatenate([west[1:], jnp.zeros_like(west[:1])], axis=0)
            north_new = jnp.concatenate([south[:, 1:], jnp.zeros_like(south[:, :1])], axis=1)
            state = jnp.concatenate([state[..., :2 * face], east_new, north_new], axis=-1)
    return state
```

```python
import jax
import jax.numpy as jnp
from jax import lax
from jax.sharding import PartitionSpec as P


F32, BF16 = jnp.float32, jnp.bfloat16
TICKS, TURN = 8, 4


def hop(array, axis, by, parity):
    nx, ny = lax.axis_size("gx"), lax.axis_size("gy")
    pairs = []
    for i in range(nx):
        for j in range(ny):
            a, b = (i + by, j) if axis == "gx" else (i, j + by)
            if (i + j) % 2 == parity and 0 <= a < nx and 0 <= b < ny:
                pairs.append((i * ny + j, a * ny + b))
    return lax.ppermute(array, ("gx", "gy"), pairs)


def dot(a, b):
    return jnp.dot(a, b, preferred_element_type=F32)


def cat(x, y):
    return jnp.concatenate([x, y], axis=1)


def on_device(maps, sources, traces):
    w = maps[0, 0]
    src = sources[0, 0]
    state = traces[0, 0]
    h = w.shape[0] // 2
    f = h // 2
    en = state[:, h:]
    got = [None, None]

    def send(tick, chain, value):
        o = value.astype(BF16)
        by = 1 if tick < TURN else -1
        parity = (tick + chain) % 2
        x = hop(o[:, :f], "gx", by, parity)
        y = hop(o[:, f:], "gy", by, parity)
        got[chain] = cat(x, y)

    def product(chain, block, constant):
        return dot(got[chain], block) + constant

    down, up = w[:h, h:], w[h:, :h]
    first = dot(state, w[:, h:]) + src[:, h:]
    c_en = dot(en, w[h:, h:]) + src[:, h:]
    q = dot(en, up)
    for tick in range(TURN):
        for chain in range(2):
            send(tick, chain, first if tick == 0 else product(chain, down, c_en))
    one, ws = got[0], got[0] + got[1]
    send(TURN, 0, dot(one, w[:h, :h]) + (src[:, :h] + q))
    c_ws = dot(ws, w[:h, :h]) + src[:, :h]
    send(TURN, 1, c_ws + q)
    c_out = cat(c_ws, dot(ws, down) + src[:, h:])
    for tick in range(TURN + 1, TICKS - 1):
        for chain in range(2):
            send(tick, chain, product(chain, up, c_ws))
    result = (dot(got[0] + got[1], w[h:]) + c_out).astype(BF16)
    return result[None, None]


def solution(mesh):
    spec = P("gx", "gy", None, None)
    return jax.shard_map(on_device, mesh=mesh, in_specs=(spec, spec, spec), out_specs=spec, check_vma=False)
```

```python
import jax
import jax.numpy as jnp
from jax import lax
from jax.sharding import PartitionSpec as P


F32, BF16 = jnp.float32, jnp.bfloat16
TICKS, TURN = 8, 4


def hop(array, axis, by, parity):
    nx, ny = lax.axis_size("gx"), lax.axis_size("gy")
    pairs = []
    for i in range(nx):
        for j in range(ny):
            a, b = (i + by, j) if axis == "gx" else (i, j + by)
            if (i + j) % 2 == parity and 0 <= a < nx and 0 <= b < ny:
                pairs.append((i * ny + j, a * ny + b))
    return lax.ppermute(array, ("gx", "gy"), pairs)


def dot(a, b):
    return jnp.dot(a, b, preferred_element_type=F32)


def cat(x, y):
    return jnp.concatenate([x, y], axis=1)


def on_device(maps, sources, traces):
    w = maps[0, 0]
    src = sources[0, 0]
    state = traces[0, 0]
    h = w.shape[0] // 2
    f = h // 2
    en = state[:, h:]
    got = [None, None]

    def send(tick, chain, x, y):
        by = 1 if tick < TURN else -1
        parity = (tick + chain) % 2
        y = hop(y, "gy", by, parity)
        x = hop(x, "gx", by, parity)
        got[chain] = (x, y)

    def send_both(tick, chain, value):
        o = value.astype(BF16)
        send(tick, chain, o[:, :f], o[:, f:])

    def product(chain, block, constant):
        return dot(cat(*got[chain]), block) + constant

    down, up = w[:h, h:], w[h:, :h]
    north = (dot(state, w[:, h + f :]) + src[:, h + f :]).astype(BF16)
    east = (dot(state, w[:, h : h + f]) + src[:, h : h + f]).astype(BF16)
    c_en = dot(en, w[h:, h:]) + src[:, h:]
    q = dot(en, up)
    for chain in range(2):
        send(0, chain, east, north)
    for tick in range(1, TURN):
        for chain in range(2):
            send_both(tick, chain, product(chain, down, c_en))
    one, two = cat(*got[0]), cat(*got[1])
    ws = one + two
    send_both(TURN, 0, dot(one, w[:h, :h]) + (src[:, :h] + q))
    c_ws = dot(ws, w[:h, :h]) + src[:, :h]
    send_both(TURN, 1, c_ws + q)
    c_out = cat(c_ws, dot(ws, down) + src[:, h:])
    for tick in range(TURN + 1, TICKS - 1):
        for chain in range(2):
            send_both(tick, chain, product(chain, up, c_ws))
    c_out = dot(got[0][0] + got[1][0], w[h : h + f]) + c_out
    result = dot(got[0][1] + got[1][1], w[h + f :]) + c_out
    result = result.astype(BF16)
    return result[None, None]


def solution(mesh):
    spec = P("gx", "gy", None, None)
    return jax.shard_map(on_device, mesh=mesh, in_specs=(spec, spec, spec), out_specs=spec, check_vma=False)
```
